32 devices in a mesh: groups: 2 (over y), dp: 4 (over x, core), mp: 4 (over z).
Axes of the slice: x: 2, y: 2, z: 4, core: 2. Of those that a mesh axis runs over, the one named last changes fastest.
Arguments:
- base_states: bfloat16 [1280, 4096], P(('groups', 'dp'), 'mp'), parts along dimension 0, may hold values from -6 to 6
- source_states: bfloat16 [1280, 4096], P(('groups', 'dp'), 'mp'), parts along dimension 0, may hold values from -6 to 6
- source_rank: int32 [1280, 1], P(('groups', 'dp')), parts along dimension 0, may hold values from 0 to 3; in each aligned block of 160 rows (0 to 159, 160 to 319, ...) at most 80 rows name the same one
- source_row: int32 [1280], P(('groups', 'dp')), parts along dimension 0, may hold values from 0 to 159
- rotation: bfloat16 [4096, 4096], P(None, 'mp'), may hold values from -0.125 to 0.125
- mask_logits: float32 [4096], P('mp'), may hold values from -8 to 8
- norm_gain: bfloat16 [4096], replicated, may hold values from 0.25 to 1.75
- gate_weight: bfloat16 [4096, 14336], P(None, 'mp'), may hold values from -0.09375 to 0.09375
- up_weight: bfloat16 [4096, 14336], P(None, 'mp'), may hold values from -0.09375 to 0.09375
- hidden_cot: bfloat16 [1280, 14336], P(('groups', 'dp'), 'mp'), parts along dimension 0, may hold values from -0.23632812 to 0.23632812
Outputs:
- rotation_grad: float32 [8192, 4096], P(('groups', 'dp'), 'mp'), parts along dimension 0
- interchanged: bfloat16 [1280, 4096], P(('groups', 'dp'), 'mp'), parts along dimension 0
The draws below stay inside these ranges and needn't reach their ends.
There are 2 independent parts, one for each index of `groups`. The reference program is written for one: setup_inputs(seed, part) draws one part's arguments, and reference() takes and returns one part's arrays. A program takes and returns all parts, laid end to end along the dimension named above; an argument that names none is the same for every part. Nothing has to cross between parts.
Inputs may be any that keep to these rules, and one draw needn't show every extreme that they name: `source_rank`: within the 160 tokens of each dp index, no dp index is named more than 80 times, and some dp index is named exactly 80 times by the tokens of some dp index.
All inputs are finite; a program needn't handle non-finite values.
Results may differ from the reference program's by a relative error of at most 0.014.
Values may be sent and summed in bfloat16 or wider, within the bound.
A program may use at most 192 MiB of HBM per device.

```python
import math
import jax
import jax.numpy as jnp
import numpy as np
from jax import lax

D = 4096
FF = 14336
TOK_DEV = 160
CAP = 80
T_ALL = 640
N_DP = 4


def with_ends(values, stream_key, low, high):
    longest = values.shape.index(max(values.shape))
    spots = []
    for shift in (0, 1):
        where = [jax.random.randint(jax.random.fold_in(stream_key, axis), (), 0, length) for axis, length in enumerate(values.shape)]
        where[longest] = (where[longest] + shift) % values.shape[longest]
        spots.append(tuple(where))
    return values.at[spots[0]].set(low).at[spots[1]].set(high)


def with_spikes(array, stream_key, source, target, parts, factor):
    def block_of(dim):
        return (jnp.arange(array.shape[dim]) // (array.shape[dim] // parts)).reshape((-1,) + (1,) * (array.ndim - 1 - dim))

    one_side = jax.random.permutation(stream_key, parts)[block_of(target)]
    other_side = (block_of(target) + parts // 2) % parts
    return jnp.where((block_of(source) == one_side) | (block_of(source) == other_side), factor * array, array)


def level_of(key, shape, pieces, smallest, top_value):
    def one(position, blocks):
        heights = jax.random.uniform(jax.random.fold_in(jax.random.fold_in(key, 6), position), (blocks,), jnp.float32, smallest / len(pieces), top_value / len(pieces))
        return jnp.repeat(jnp.exp(heights), shape[position] // blocks).reshape((-1,) + (1,) * (len(shape) - position - 1))

    loudness = one(*pieces[0])
    for cut in pieces[1:]:
        loudness = loudness * one(*cut)
    return loudness


def routed_block(own_key, own, number, rows, count, top, most, lean):
    sequence = jax.random.permutation(own_key, count)
    heavy_load, usual = load_shares(count, rows * top, most, lean, True), load_shares(count, rows * top, most, lean, False)
    places = jnp.arange(count)

    def named(tallies, turn):
        used = int((tallies > 0).sum())
        fixed = max(1, used // 4)
        passed = fixed + (places - fixed + turn * (used - fixed)) % max(1, count - fixed)
        return jnp.zeros((count,), jnp.int32).at[sequence[jnp.where(places < fixed, places, passed)]].set(jnp.asarray(tallies, jnp.int32))

    tallies = jnp.where(number % 4 == 0, named(heavy_load, number // 4), named(usual, number - number // 4 - 1))
    mixed = jax.random.permutation(jax.random.fold_in(own, 3), count)
    source_of, receiver = mixed[0:count // 2 * 2:2], mixed[1:count // 2 * 2:2]
    slack = jnp.minimum(tallies[source_of] - 1, most - tallies[receiver]) // 2
    slack = jnp.where((source_of == sequence[0]) | (receiver == sequence[0]) | (tallies[receiver] == 0), 0, jnp.maximum(slack, 0))
    passed = jax.random.randint(jax.random.fold_in(own, 4), (count // 2,), 0, 1 << 20) % (slack + 1)
    tallies = tallies.at[source_of].add(-passed).at[receiver].add(passed)
    members = jnp.searchsorted(jnp.cumsum(tallies), jnp.arange(rows * top), side="right").astype(jnp.int32)
    table = members.reshape(top, rows).T
    table = table[jax.random.permutation(jax.random.fold_in(own, 1), rows)]
    turn = jax.random.randint(jax.random.fold_in(own, 2), (rows, 1), 0, top)
    return jnp.take_along_axis(table, (jnp.arange(top)[None, :] + turn) % top, axis=1)


def load_shares(number_of, total, most, skew, full):
    portions = [(1 << 20) // math.isqrt(grade ** skew) + 1 for grade in range(1, number_of + 1)]
    largest = most if full else min(most, max(-(-total // number_of), total * portions[0] // sum(portions)))
    least = 1 if total - largest >= number_of - 1 else 0
    counts, surplus = [largest] + [least] * (number_of - 1), total - largest - least * (number_of - 1)
    while surplus > 0:
        movable = [i for i in range(1, number_of) if counts[i] < largest] or [i for i in range(1, number_of) if counts[i] < most]
        whole, budget = sum([portions[i] for i in movable]), surplus
        for i in movable:
            extra = min(most - counts[i], max(1, budget * portions[i] // whole), surplus)
            counts[i] = counts[i] + extra
            surplus = surplus - extra
    return np.array(counts)


def centred(own_key, extent, scale, bound, pieces=(), kind=jnp.bfloat16):
    array = scale * jax.random.normal(own_key, extent, jnp.float32)
    if pieces:
        array = array * level_of(own_key, extent, pieces, -0.22, 0.18)
    return jnp.clip(array, -bound, bound).astype(kind)


def gaussian_with(own_key, extent, width, limit, split, heavy, dtype=jnp.bfloat16):
    result = width * jax.random.normal(own_key, extent, jnp.float32)
    if split:
        result = result * level_of(own_key, extent, split, -0.22, 0.18)
    return jnp.clip(with_spikes(result, jax.random.fold_in(own_key, 3), *heavy), -limit, limit).astype(dtype)


def setup_inputs(seed: int = 0, part: int = 0) -> dict:
    splits = jax.random.split(jax.random.key(seed), 11)
    own_keys = jax.random.split(jax.random.fold_in(splits[10], part), 11)
    base_states = centred(own_keys[0], (T_ALL, D), 1.0, 6.0, ((0, 4), (1, 4)))
    source_states = centred(own_keys[1], (T_ALL, D), 1.0, 6.0, ((0, 4), (1, 4)))
    source_rank_keys = jax.random.split(jax.random.fold_in(own_keys[2], 1), T_ALL // TOK_DEV)
    source_rank_turns = jax.random.permutation(jax.random.fold_in(own_keys[2], 3), T_ALL // TOK_DEV)
    source_rank = jax.vmap(lambda own, number: routed_block(jax.random.fold_in(own_keys[2], 2), own, number, TOK_DEV, N_DP, 1, CAP, 1))(source_rank_keys, source_rank_turns).reshape((T_ALL, 1))
    source_row = with_ends(jax.random.randint(own_keys[3], (T_ALL,), 0, TOK_DEV), jax.random.fold_in(own_keys[3], 1), 0, TOK_DEV - 1).astype(jnp.int32)
    rotation = gaussian_with(splits[4], (D, D), D ** -0.5, 0.125, ((1, 4),), (1, 0, 4, 2.0))
    mask_logits = centred(splits[5], (D,), 2.0, 8.0, ((0, 4),), jnp.float32)
    norm_gain = jnp.clip(1.0 + 0.15 * jax.random.normal(splits[6], (D,), jnp.float32), 0.25, 1.75).astype(jnp.bfloat16)
    gate_weight = centred(splits[7], (D, FF), D ** -0.5, 0.09375, ((1, 4),))
    up_weight = centred(splits[8], (D, FF), D ** -0.5, 0.09375, ((1, 4),))
    hidden_cot = centred(own_keys[9], (T_ALL, FF), (T_ALL ** -0.5), 0.23632812, ((0, 4), (1, 4)))
    return dict(base_states=base_states, source_states=source_states, source_rank=source_rank, source_row=source_row, rotation=rotation, mask_logits=mask_logits, norm_gain=norm_gain, gate_weight=gate_weight, up_weight=up_weight, hidden_cot=hidden_cot)


def reference(base_states, source_states, source_rank, source_row, rotation, mask_logits, norm_gain, gate_weight, up_weight, hidden_cot):
    flat_index = (source_rank[:, 0] * TOK_DEV + source_row).astype(jnp.int32)
    paired = jnp.take(source_states, flat_index, axis=0)
    diff = (paired.astype(jnp.float32) - base_states.astype(jnp.float32)).astype(jnp.bfloat16)
    mask = jax.nn.sigmoid(mask_logits)
    coords = jnp.dot(diff, rotation, preferred_element_type=jnp.float32)
    weighted = (mask[None, :] * coords).astype(jnp.bfloat16)
    moved = jnp.dot(weighted, rotation.T, preferred_element_type=jnp.float32)
    interchanged = (base_states.astype(jnp.float32) + moved).astype(jnp.bfloat16)
    states = interchanged.astype(jnp.float32)
    gain_f = norm_gain.astype(jnp.float32)[None, :]
    recip = lax.rsqrt(lax.optimization_barrier(jnp.mean(states * states, axis=1, keepdims=True)) + 1e-05)
    normed = (states * recip * gain_f).astype(jnp.bfloat16)
    gate = jnp.dot(normed, gate_weight, preferred_element_type=jnp.float32)
    up_val = jnp.dot(normed, up_weight, preferred_element_type=jnp.float32)
    sigm = jax.nn.sigmoid(gate)
    cotan = hidden_cot.astype(jnp.float32)
    dgate = (cotan * up_val * sigm * (1.0 + gate * (1.0 - sigm))).astype(jnp.bfloat16)
    dup_val = (cotan * gate * sigm).astype(jnp.bfloat16)
    dnormed = jnp.dot(dgate, gate_weight.T, preferred_element_type=jnp.float32) + jnp.dot(dup_val, up_weight.T, preferred_element_type=jnp.float32)
    scaled = gain_f * dnormed
    stat = lax.optimization_barrier(jnp.sum(scaled * states, axis=1, keepdims=True))
    dinter = (recip * scaled - states * recip * recip * recip * stat / D).astype(jnp.bfloat16)
    coupled = (mask[None, :] * jnp.dot(dinter, rotation, preferred_element_type=jnp.float32)).astype(jnp.bfloat16)
    rotation_grad = jnp.dot(dinter.T, weighted, preferred_element_type=jnp.float32) + jnp.dot(diff.T, coupled, preferred_element_type=jnp.float32)
    return (rotation_grad, interchanged)
```

```python
import functools

import jax
import jax.numpy as jnp
from jax import lax
from jax.experimental import pallas as pl
from jax.experimental.pallas import tpu as pltpu
from jax.sharding import PartitionSpec as P

BF = jnp.bfloat16
F32 = jnp.float32
CHUNKS = 2
TILE = 256


def contract_first(left, right):
    return lax.dot_general(
        left, right, (((0,), (0,)), ((), ())), preferred_element_type=F32
    )


def contract_last(left, right):
    return lax.dot_general(
        left, right, (((1,), (1,)), ((), ())), preferred_element_type=F32
    )


def send(src, dst, ssem, rsem, axis, dev):
    return pltpu.make_async_remote_copy(
        src_ref=src,
        dst_ref=dst,
        send_sem=ssem,
        recv_sem=rsem,
        device_id={axis: dev},
        device_id_type=pl.DeviceIdType.MESH,
    )


def rows_of(chunk, tokens):
    size = tokens // CHUNKS
    return pl.ds(chunk * size, size)


def greet(me, n, dp):
    barrier = pltpu.get_barrier_semaphore()
    for r in (1, 2, 3):
        pl.semaphore_signal(
            barrier, inc=1, device_id={"dp": partner(dp, r)}, device_id_type=pl.DeviceIdType.MESH
        )

    @pl.when(me > 0)
    def _():
        pl.semaphore_signal(
            barrier, inc=1, device_id={"mp": me - 1}, device_id_type=pl.DeviceIdType.MESH
        )

    @pl.when(me < n - 1)
    def _():
        pl.semaphore_signal(
            barrier, inc=1, device_id={"mp": me + 1}, device_id_type=pl.DeviceIdType.MESH
        )

    pl.semaphore_wait(barrier, 3 + jnp.minimum(me, 1) + jnp.minimum(n - 1 - me, 1))


def partner(dp, r):
    low = dp % 2
    high = dp // 2
    if r % 2:
        low = 1 - low
    if r // 2:
        high = 1 - high
    return high * 2 + low


def line_gather(buf, ssem, rsem, me, n, tokens, use):
    def right(k, c):
        view = buf.at[me - k, rows_of(c, tokens)]
        return send(view, view, ssem.at[0, k, c], rsem.at[0, k, c], "mp", me + 1)

    def left(k, c):
        view = buf.at[me + k, rows_of(c, tokens)]
        return send(view, view, ssem.at[1, k, c], rsem.at[1, k, c], "mp", me - 1)

    def arrived_right(k, c):
        view = buf.at[me - 1 - k, rows_of(c, tokens)]
        return send(view, view, ssem.at[0, k, c], rsem.at[0, k, c], "mp", me + 1)

    def arrived_left(k, c):
        view = buf.at[me + 1 + k, rows_of(c, tokens)]
        return send(view, view, ssem.at[1, k, c], rsem.at[1, k, c], "mp", me - 1)

    for k in range(n):
        for c in range(CHUNKS):
            if k > 0:
                pl.when(me - k >= 0)(lambda: arrived_right(k - 1, c).wait_recv())
            if k < n - 1:
                pl.when((me - k >= 0) & (me < n - 1))(lambda: right(k, c).start())
            if k > 0:
                pl.when(me + k <= n - 1)(lambda: arrived_left(k - 1, c).wait_recv())
            if k < n - 1:
                pl.when((me + k <= n - 1) & (me > 0))(lambda: left(k, c).start())
        if k == 0:
            use(me)
        else:
            pl.when(me - k >= 0)(lambda: use(me - k))
            pl.when(me + k <= n - 1)(lambda: use(me + k))
    for k in range(n - 1):
        for c in range(CHUNKS):
            pl.when((me - k >= 0) & (me < n - 1))(lambda: right(k, c).wait_send())
            pl.when((me + k <= n - 1) & (me > 0))(lambda: left(k, c).wait_send())


def line_reduce(part, sums, ssem, rsem, total, me, n, tokens):
    flip = (me * 2) // n
    sign = 1 - 2 * flip
    v = me + flip * (n - 1 - 2 * me)

    def real(j):
        return j + flip * (n - 1 - 2 * j)

    def hop(stream, j, c):
        way = flip if stream == 0 else 1 - flip
        to = me + sign if stream == 0 else me - sign
        view = sums.at[way, real(j), rows_of(c, tokens)]
        return send(view, view, ssem.at[way, real(j), c], rsem.at[way, real(j), c], "mp", to)

    def step(stream, j, c):
        way = flip if stream == 0 else 1 - flip
        rows = rows_of(c, tokens)
        first = (v == 0) if stream == 0 else (v == n - 1)
        sender = (v < j) if stream == 0 else (v > j)

        @pl.when(sender & first)
        def _():
            sums[way, real(j), rows] = part[real(j), rows]

        @pl.when(sender & jnp.logical_not(first))
        def _():
            hop(stream, j, c).wait_recv()
            sums[way, real(j), rows] = (
                sums[way, real(j), rows].astype(F32) + part[real(j), rows].astype(F32)
            ).astype(BF)

        pl.when(sender)(lambda: hop(stream, j, c).start())

    for s in range(n - 1):
        for stream, j in ((0, n - 1 - s), (1, s)):
            for c in range(CHUNKS):
                step(stream, j, c)
    total[...] = part[me].astype(F32)
    for way, there, frm in ((0, me > 0, me - 1), (1, me < n - 1, me + 1)):

        @pl.when(there)
        def _():
            for c in range(CHUNKS):
                view = sums.at[way, me, rows_of(c, tokens)]
                send(view, view, ssem.at[way, me, c], rsem.at[way, me, c], "mp", frm).wait_recv()
            total[...] += sums[way, me].astype(F32)

    for s in range(n - 1):
        for stream, j in ((0, n - 1 - s), (1, s)):
            sender = (v < j) if stream == 0 else (v > j)
            for c in range(CHUNKS):
                pl.when(sender)(lambda: hop(stream, j, c).wait_send())


def times_rotation(left, rot, block, acc):
    shard = left.shape[1]

    def body(i, carry):
        cols = pl.ds(pl.multiple_of(i * TILE, TILE), TILE)
        rows = pl.ds(pl.multiple_of(block * shard, shard), shard)
        acc[:, cols] += jnp.dot(left, rot[rows, cols], preferred_element_type=F32)
        return carry

    lax.fori_loop(0, acc.shape[1] // TILE, body, 0)


def front_kernel(
    n,
    src,
    base,
    index,
    logits,
    rot_hbm,
    weighted,
    diff_full,
    inter_full,
    inter_own,
    rot,
    pool,
    part,
    sums,
    acc,
    rot_sem,
    pool_s,
    pool_r,
    gd_s,
    gd_r,
    red_s,
    red_r,
    gi_s,
    gi_r,
):
    me = lax.axis_index("mp")
    dp = lax.axis_index("dp")
    tokens, width = src.shape
    load = pltpu.make_async_copy(rot_hbm, rot, rot_sem)
    load.start()
    greet(me, n, dp)

    def across(i, frm, to):
        return send(frm, pool.at[to[0]], pool_s.at[i], pool_r.at[i], "dp", to[1])

    near, far, both = partner(dp, 1), partner(dp, 2), partner(dp, 3)
    one = across(0, src, (2, far))
    two = across(1, src, (1, near))
    one.start()
    two.start()
    pool[0] = src[...]
    one.wait_recv()
    three = across(2, pool.at[2], (3, near))
    three.start()
    owner = index[...]
    lane = lax.broadcasted_iota(jnp.int32, (tokens, tokens), 1)

    def pick(slot, who):
        hit = (owner == lane + who * tokens).astype(F32).astype(BF)
        return jnp.dot(hit, pool[slot], preferred_element_type=F32)

    acc[...] = pick(0, dp) + pick(2, far)
    two.wait_recv()
    acc[...] += pick(1, near)
    three.wait_recv()
    acc[...] += pick(3, both)
    diff_full[me] = (acc[...] - base[...].astype(F32)).astype(BF)
    acc[...] = jnp.zeros_like(acc)

    first = [True]

    def use(j):
        if first[0]:
            first[0] = False
            load.wait()
        times_rotation(diff_full[j], rot, j, acc)

    line_gather(diff_full, gd_s, gd_r, me, n, tokens, use)
    weighted[...] = (jax.nn.sigmoid(logits[...]) * acc[...]).astype(BF)

    def back(i, carry):
        per = width // TILE
        rows = pl.ds(pl.multiple_of(i * TILE, TILE), TILE)
        cols = pl.ds(pl.multiple_of((i % per) * TILE, TILE), TILE)
        part[i // per, :, cols] = contract_last(weighted[...], rot[rows, :]).astype(BF)
        return carry

    lax.fori_loop(0, rot.shape[0] // TILE, back, 0)
    line_reduce(part, sums, red_s, red_r, acc, me, n, tokens)
    mine = (base[...].astype(F32) + acc[...]).astype(BF)
    inter_full[me] = mine
    inter_own[...] = mine
    line_gather(inter_full, gi_s, gi_r, me, n, tokens, lambda j: None)
    one.wait_send()
    two.wait_send()
    three.wait_send()


def recip_of(inter, n):
    tokens, width = inter.shape[1:]
    square = jnp.zeros((tokens, 1), F32)
    for j in range(n):
        block = inter[j].astype(F32)
        square = square + jnp.sum(block * block, axis=1, keepdims=True)
    return lax.rsqrt(square / (n * width) + 1e-05)


def ffn_kernel(n, inter, gain, wg, wu, cot, out, normed, total):
    tokens, width = inter.shape[1:]
    step = pl.program_id(0)

    @pl.when(step == 0)
    def _():
        recip = recip_of(inter, n)
        for j in range(n):
            cols = pl.ds(j * width, width)
            scale = gain[:, cols].astype(F32)
            normed[:, cols] = (inter[j].astype(F32) * recip * scale).astype(BF)
        total[...] = jnp.zeros_like(total)

    gate = jnp.dot(normed[...], wg[...], preferred_element_type=F32)
    up = jnp.dot(normed[...], wu[...], preferred_element_type=F32)
    sig = jax.nn.sigmoid(gate)
    cotan = cot[...].astype(F32)
    dgate = (cotan * up * sig * (1.0 + gate * (1.0 - sig))).astype(BF)
    dup = (cotan * gate * sig).astype(BF)
    for i in range(n * width // 512):
        rows = pl.ds(i * 512, 512)
        total[:, rows] += contract_last(dgate, wg[rows, :]) + contract_last(dup, wu[rows, :])

    @pl.when(step == pl.num_programs(0) - 1)
    def _():
        for j in range(n):
            out[j] = total[:, pl.ds(j * width, width)].astype(BF)


def back_kernel(
    n,
    part,
    inter,
    gain,
    logits,
    rot_hbm,
    dinter_all,
    coupled_all,
    rot,
    sums,
    dn,
    dinter,
    acc,
    stat,
    rot_sem,
    red_s,
    red_r,
    ga_s,
    ga_r,
    ex_s,
    ex_r,
    co_s,
    co_r,
):
    me = lax.axis_index("mp")
    dp = lax.axis_index("dp")
    tokens, width = part.shape[1:]
    load = pltpu.make_async_copy(rot_hbm, rot, rot_sem)
    load.start()
    greet(me, n, dp)
    line_reduce(part, sums, red_s, red_r, acc, me, n, tokens)
    dn[me] = acc[...].astype(BF)
    stat[...] = jnp.zeros_like(stat)

    def use(j):
        scaled = gain[j].astype(F32) * dn[j].astype(F32)
        stat[...] += jnp.sum(scaled * inter[j].astype(F32), axis=1, keepdims=True)

    line_gather(dn, ga_s, ga_r, me, n, tokens, use)
    recip = recip_of(inter, n)
    coef = recip * recip * recip * stat[...] / (n * width)

    copies = []
    for j in range(n):
        scaled = gain[j].astype(F32) * dn[j].astype(F32)
        dinter[j] = (recip * scaled - inter[j].astype(F32) * coef).astype(BF)
    for r in (2, 3, 1):
        to = partner(dp, r)
        copy = send(dinter.at[to], dinter_all.at[r], ex_s.at[r], ex_r.at[r], "dp", to)
        copy.start()
        copies.append(copy)
    dinter_all[0] = dinter[dp]
    load.wait()
    acc[...] = jnp.zeros_like(acc)
    for j in range(n):
        times_rotation(dinter[j], rot, j, acc)
    coupled_all[0] = (jax.nn.sigmoid(logits[...]) * acc[...]).astype(BF)
    near, far = partner(dp, 1), partner(dp, 2)
    own = coupled_all.at[0]
    one = send(own, coupled_all.at[2], co_s.at[0], co_r.at[0], "dp", far)
    two = send(own, coupled_all.at[1], co_s.at[1], co_r.at[1], "dp", near)
    one.start()
    two.start()
    one.wait_recv()
    three = send(coupled_all.at[2], coupled_all.at[3], co_s.at[2], co_r.at[2], "dp", near)
    three.start()
    for copy in copies:
        copy.wait_recv()
    two.wait_recv()
    three.wait_recv()
    for copy in copies + [one, two, three]:
        copy.wait_send()


def grad_kernel(count, *refs):
    dinter, coupled = refs[0], refs[1]
    weighted = refs[2 : 2 + count]
    diff = refs[2 + count : 2 + 2 * count]
    out = refs[-1]
    rows = pl.program_id(0)
    acc = jnp.zeros(out.shape, F32)
    for r in range(count):
        acc = acc + contract_first(dinter[r], weighted[r][...])
        acc = acc + contract_first(diff[r][...], coupled[r])
    out[...] = acc


def vmem():
    return pl.BlockSpec(memory_space=pltpu.VMEM)


def anywhere():
    return pl.BlockSpec(memory_space=pl.ANY)


def dma(*shape):
    return pltpu.SemaphoreType.DMA(shape)


def fast(
    n,
    base_states,
    source_states,
    source_rank,
    source_row,
    rotation,
    mask_logits,
    norm_gain,
    gate_weight,
    up_weight,
    hidden_cot,
):
    tokens, width = base_states.shape
    hidden = gate_weight.shape[1]
    full = rotation.shape[0]
    peers = 4
    index = source_rank * tokens + source_row[:, None]
    logits = mask_logits[None, :]
    whole = jax.ShapeDtypeStruct((n, tokens, width), BF)
    one = jax.ShapeDtypeStruct((tokens, width), BF)
    line = (2, n - 1, CHUNKS)
    weighted, diff_full, inter_full, interchanged = pl.pallas_call(
        functools.partial(front_kernel, n),
        out_shape=(one, whole, whole, one),
        in_specs=[vmem()] * 4 + [anywhere()],
        out_specs=(vmem(),) * 4,
        scratch_shapes=[
            pltpu.VMEM((full, width), BF),
            pltpu.VMEM((peers, tokens, width), BF),
            pltpu.VMEM((n, tokens, width), BF),
            pltpu.VMEM((2, n, tokens, width), BF),
            pltpu.VMEM((tokens, width), F32),
            pltpu.SemaphoreType.DMA,
            dma(3),
            dma(3),
            dma(*line),
            dma(*line),
            dma(2, n, CHUNKS),
            dma(2, n, CHUNKS),
            dma(*line),
            dma(*line),
        ],
        compiler_params=pltpu.CompilerParams(collective_id=0, has_side_effects=True),
        name="front",
    )(source_states, base_states, index, logits, rotation)

    dp = lax.axis_index("dp")
    weights_of = [weighted]
    diffs_of = [diff_full[dp]]
    for r in range(1, peers):
        perm = [(i, i ^ r) for i in range(peers)]
        weights_of.append(lax.ppermute(weighted, "dp", perm))
        diffs_of.append(lax.ppermute(diff_full[dp ^ r], "dp", perm))

    block = 512 if hidden % 512 == 0 else hidden
    part = pl.pallas_call(
        functools.partial(ffn_kernel, n),
        out_shape=whole,
        grid=(hidden // block,),
        in_specs=[
            pl.BlockSpec((n, tokens, width), lambda i: (0, 0, 0)),
            pl.BlockSpec((1, full), lambda i: (0, 0)),
            pl.BlockSpec((full, block), lambda i: (0, i)),
            pl.BlockSpec((full, block), lambda i: (0, i)),
            pl.BlockSpec((tokens, block), lambda i: (0, i)),
        ],
        out_specs=pl.BlockSpec((n, tokens, width), lambda i: (0, 0, 0)),
        scratch_shapes=[pltpu.VMEM((tokens, full), BF), pltpu.VMEM((tokens, full), F32)],
        cost_estimate=pl.CostEstimate(
            flops=8 * tokens * full * hidden,
            bytes_accessed=4 * full * hidden,
            transcendentals=tokens * hidden,
        ),
        name="ffn",
    )(inter_full, norm_gain[None, :], gate_weight, up_weight, hidden_cot)

    dinter_all, coupled_all = pl.pallas_call(
        functools.partial(back_kernel, n),
        out_shape=(jax.ShapeDtypeStruct((peers, tokens, width), BF),) * 2,
        in_specs=[vmem()] * 4 + [anywhere()],
        out_specs=(vmem(),) * 2,
        scratch_shapes=[
            pltpu.VMEM((full, width), BF),
            pltpu.VMEM((2, n, tokens, width), BF),
            pltpu.VMEM((n, tokens, width), BF),
            pltpu.VMEM((n, tokens, width), BF),
            pltpu.VMEM((tokens, width), F32),
            pltpu.VMEM((tokens, 1), F32),
            pltpu.SemaphoreType.DMA,
            dma(2, n, CHUNKS),
            dma(2, n, CHUNKS),
            dma(*line),
            dma(*line),
            dma(peers),
            dma(peers),
            dma(3),
            dma(3),
        ],
        compiler_params=pltpu.CompilerParams(collective_id=1, has_side_effects=True),
        name="back",
    )(part, inter_full, norm_gain.reshape(n, 1, width), logits, rotation)

    rows = 256
    rotation_grad = pl.pallas_call(
        functools.partial(grad_kernel, peers),
        out_shape=jax.ShapeDtypeStruct((full // peers, width), F32),
        grid=(full // peers // rows,),
        in_specs=[
            pl.BlockSpec((peers, tokens, rows), lambda i: (0, 0, i)),
            pl.BlockSpec((peers, tokens, width), lambda i: (0, 0, 0)),
        ]
        + [pl.BlockSpec((tokens, width), lambda i: (0, 0))] * peers
        + [pl.BlockSpec((tokens, rows), lambda i: (0, i))] * peers,
        out_specs=pl.BlockSpec((rows, width), lambda i: (i, 0)),
        name="grad",
    )(dinter_all, coupled_all, *weights_of, *diffs_of)
    return (rotation_grad, interchanged)


def plain(
    base_states,
    source_states,
    source_rank,
    source_row,
    rotation,
    mask_logits,
    norm_gain,
    gate_weight,
    up_weight,
    hidden_cot,
):
    tokens = base_states.shape[0]
    width = rotation.shape[0]
    ranks_of = source_rank[:, 0]
    everyone = lax.all_gather(source_states, "dp", axis=0, tiled=True)
    paired = jnp.take(everyone, ranks_of * tokens + source_row, axis=0)
    diff_local = (paired.astype(jnp.float32) - base_states.astype(jnp.float32)).astype(jnp.bfloat16)
    diff_full = lax.all_gather(diff_local, "mp", axis=1, tiled=True)
    mask = jax.nn.sigmoid(mask_logits)[None, :]
    coords = jnp.dot(diff_full, rotation, preferred_element_type=jnp.float32)
    weighted = (mask * coords).astype(jnp.bfloat16)
    moved = lax.psum_scatter(
        contract_last(rotation, weighted), "mp", scatter_dimension=0, tiled=True
    ).T
    interchanged = (base_states.astype(jnp.float32) + moved).astype(jnp.bfloat16)
    full_rows = lax.all_gather(interchanged, "mp", axis=1, tiled=True)
    states = full_rows.astype(jnp.float32)
    gain_f = norm_gain.astype(jnp.float32)[None, :]
    recip = lax.rsqrt(jnp.mean(states * states, axis=1, keepdims=True) + 1e-05)
    normed = (states * recip * gain_f).astype(jnp.bfloat16)
    gate = jnp.dot(normed, gate_weight, preferred_element_type=jnp.float32)
    up_val = jnp.dot(normed, up_weight, preferred_element_type=jnp.float32)
    sigm = jax.nn.sigmoid(gate)
    cotan = hidden_cot.astype(jnp.float32)
    dgate = (cotan * up_val * sigm * (1.0 + gate * (1.0 - sigm))).astype(jnp.bfloat16)
    dup_val = (cotan * gate * sigm).astype(jnp.bfloat16)
    partial_grad = contract_last(dgate, gate_weight) + contract_last(dup_val, up_weight)
    dnormed = lax.psum(partial_grad, "mp")
    scaled = gain_f * dnormed
    stat = jnp.sum(scaled * states, axis=1, keepdims=True)
    dinter = (recip * scaled - states * recip * recip * recip * stat / width).astype(jnp.bfloat16)
    coupled = (mask * jnp.dot(dinter, rotation, preferred_element_type=jnp.float32)).astype(
        jnp.bfloat16
    )
    rotation_grad = lax.psum_scatter(
        (contract_first(dinter, weighted) + contract_first(diff_full, coupled)).astype(
            jnp.bfloat16
        ),
        "dp",
        scatter_dimension=0,
        tiled=True,
    ).astype(jnp.float32)
    return (rotation_grad, interchanged)


def solution(mesh):
    n = mesh.shape["mp"]

    def shards(*args):
        width = args[0].shape[1]
        tokens = args[0].shape[0]
        full = args[4].shape[0]
        fits = (
            width % TILE == 0
            and mesh.shape["dp"] == 4
            and 1 < n <= 8
            and n * width == full
            and full // 4 == width
            and tokens % (16 * CHUNKS) == 0
        )
        if fits:
            return fast(n, *args)
        return plain(*args)

    placed = (
        P(("groups", "dp"), "mp"),
        P(("groups", "dp"), "mp"),
        P(("groups", "dp"), None),
        P(("groups", "dp")),
        P(None, "mp"),
        P("mp"),
        P(),
        P(None, "mp"),
        P(None, "mp"),
        P(("groups", "dp"), "mp"),
    )
    return jax.shard_map(
        shards,
        mesh=mesh,
        in_specs=placed,
        out_specs=(P(("groups", "dp"), "mp"), P(("groups", "dp"), "mp")),
        check_vma=False,
    )
```

```python
import functools

import jax
import jax.numpy as jnp
from jax import lax
from jax.experimental import pallas as pl
from jax.experimental.pallas import tpu as pltpu
from jax.sharding import PartitionSpec as P

BF = jnp.bfloat16
F32 = jnp.float32
CHUNKS = 2
TILE = 512


def contract_first(left, right):
    return lax.dot_general(
        left, right, (((0,), (0,)), ((), ())), preferred_element_type=F32
    )


def contract_last(left, right):
    return lax.dot_general(
        left, right, (((1,), (1,)), ((), ())), preferred_element_type=F32
    )


def send(src, dst, ssem, rsem, axis, dev):
    return pltpu.make_async_remote_copy(
        src_ref=src,
        dst_ref=dst,
        send_sem=ssem,
        recv_sem=rsem,
        device_id={axis: dev},
        device_id_type=pl.DeviceIdType.MESH,
    )


def rows_of(chunk, tokens):
    size = tokens // CHUNKS
    return pl.ds(chunk * size, size)


def greet(me, n, dp):
    barrier = pltpu.get_barrier_semaphore()
    for r in (1, 2, 3):
        pl.semaphore_signal(
            barrier, inc=1, device_id={"dp": partner(dp, r)}, device_id_type=pl.DeviceIdType.MESH
        )

    @pl.when(me > 0)
    def _():
        pl.semaphore_signal(
            barrier, inc=1, device_id={"mp": me - 1}, device_id_type=pl.DeviceIdType.MESH
        )

    @pl.when(me < n - 1)
    def _():
        pl.semaphore_signal(
            barrier, inc=1, device_id={"mp": me + 1}, device_id_type=pl.DeviceIdType.MESH
        )

    pl.semaphore_wait(barrier, 3 + jnp.minimum(me, 1) + jnp.minimum(n - 1 - me, 1))


def partner(dp, r):
    low = dp % 2
    high = dp // 2
    if r % 2:
        low = 1 - low
    if r // 2:
        high = 1 - high
    return high * 2 + low


def line_gather(buf, ssem, rsem, me, n, tokens, use):
    def hop(way, k, c):
        shard, to = (me - k, me + 1) if way == 0 else (me + k, me - 1)
        view = buf.at[shard, rows_of(c, tokens)]
        return send(view, view, ssem.at[way, k, c], rsem.at[way, k, c], "mp", to)

    def arrival(way, k, c):
        shard, frm = (me - 1 - k, me - 1) if way == 0 else (me + 1 + k, me + 1)
        view = buf.at[shard, rows_of(c, tokens)]
        return send(view, view, ssem.at[way, k, c], rsem.at[way, k, c], "mp", frm)

    def sends(way, k):
        if way == 0:
            return (me - k >= 0) & (me < n - 1)
        return (me + k <= n - 1) & (me > 0)

    def step(c, k):
        here = (me - k >= 0, me + k <= n - 1)
        for way in (0, 1):
            if k > 0:
                pl.when(here[way])(lambda: arrival(way, k - 1, c).wait_recv())
            if k < n - 1:
                pl.when(sends(way, k))(lambda: hop(way, k, c).start())
        if k == 0:
            use(c, me)
        else:
            pl.when(here[0])(lambda: use(c, me - k))
            pl.when(here[1])(lambda: use(c, me + k))

    def drain():
        for k in range(n - 1):
            for c in range(CHUNKS):
                for way in (0, 1):
                    pl.when(sends(way, k))(lambda: hop(way, k, c).wait_send())

    return step, drain


def line_reduce(part, sums, ssem, rsem, total, me, n, tokens, prepare):
    flip = (me * 2) // n
    sign = 1 - 2 * flip
    v = me + flip * (n - 1 - 2 * me)

    def real(j):
        return j + flip * (n - 1 - 2 * j)

    def hop(stream, j, c):
        way = flip if stream == 0 else 1 - flip
        to = me + sign if stream == 0 else me - sign
        view = sums.at[way, real(j), rows_of(c, tokens)]
        return send(view, view, ssem.at[way, real(j), c], rsem.at[way, real(j), c], "mp", to)

    def one(stream, j, c):
        way = flip if stream == 0 else 1 - flip
        rows = rows_of(c, tokens)
        first = (v == 0) if stream == 0 else (v == n - 1)
        sender = (v < j) if stream == 0 else (v > j)

        @pl.when(sender & first)
        def _():
            sums[way, real(j), rows] = part[real(j), rows]

        @pl.when(sender & jnp.logical_not(first))
        def _():
            hop(stream, j, c).wait_recv()
            sums[way, real(j), rows] = (
                sums[way, real(j), rows].astype(F32) + part[real(j), rows].astype(F32)
            ).astype(BF)

        pl.when(sender)(lambda: hop(stream, j, c).start())

    def step(c, s):
        for stream, j in ((0, n - 1 - s), (1, s)):
            if prepare is not None and s <= n - 1 - s and (stream == 0 or s < n - 1 - s):
                prepare(c, real(j))
            one(stream, j, c)

    def finish(c):
        rows = rows_of(c, tokens)
        total[rows] = part[me, rows].astype(F32)
        for way, there, frm in ((0, me > 0, me - 1), (1, me < n - 1, me + 1)):

            @pl.when(there)
            def _():
                view = sums.at[way, me, rows]
                send(view, view, ssem.at[way, me, c], rsem.at[way, me, c], "mp", frm).wait_recv()
                total[rows] += sums[way, me, rows].astype(F32)

    def drain():
        for s in range(n - 1):
            for stream, j in ((0, n - 1 - s), (1, s)):
                sender = (v < j) if stream == 0 else (v > j)
                for c in range(CHUNKS):
                    pl.when(sender)(lambda: hop(stream, j, c).wait_send())

    return step, finish, drain


def times_rotation(left, rot, block, acc, rows):
    shard = left.shape[1]

    def body(i, carry):
        cols = pl.ds(pl.multiple_of(i * TILE, TILE), TILE)
        depth = pl.ds(pl.multiple_of(block * shard, shard), shard)
        acc[rows, cols] += jnp.dot(left, rot[depth, cols], preferred_element_type=F32)
        return carry

    lax.fori_loop(0, acc.shape[1] // TILE, body, 0)


def front_kernel(
    n,
    src,
    base,
    index,
    logits,
    rot_hbm,
    weighted_all,
    diff_all,
    inter_full,
    inter_own,
    rot,
    pool,
    diff_full,
    weighted,
    part,
    sums,
    acc,
    rot_sem,
    own_sem,
    pool_s,
    pool_r,
    gd_s,
    gd_r,
    red_s,
    red_r,
    gi_s,
    gi_r,
    di_s,
    di_r,
    we_s,
    we_r,
):
    me = lax.axis_index("mp")
    dp = lax.axis_index("dp")
    tokens, width = src.shape
    load = pltpu.make_async_copy(rot_hbm, rot, rot_sem)
    load.start()
    greet(me, n, dp)

    def across(i, frm, to):
        return send(frm, pool.at[to[0]], pool_s.at[i], pool_r.at[i], "dp", to[1])

    near, far, both = partner(dp, 1), partner(dp, 2), partner(dp, 3)
    one = across(0, src, (2, far))
    two = across(1, src, (1, near))
    one.start()
    two.start()
    owner = index[...]
    lane = lax.broadcasted_iota(jnp.int32, (tokens, tokens), 1)

    def pick(rows_in, who):
        hit = (owner == lane + who * tokens).astype(F32).astype(BF)
        return jnp.dot(hit, rows_in, preferred_element_type=F32)

    acc[...] = pick(src[...], dp)
    two.wait_recv()
    acc[...] += pick(pool[1], near)
    one.wait_recv()
    three = across(2, pool.at[2], (3, near))
    three.start()
    acc[...] += pick(pool[2], far)
    three.wait_recv()
    acc[...] += pick(pool[3], both)
    diff_full[me] = (acc[...] - base[...].astype(F32)).astype(BF)
    acc[...] = jnp.zeros_like(acc)

    waited = []

    def use(c, j):
        if not waited:
            waited.append(True)
            load.wait()
        rows = rows_of(c, tokens)
        times_rotation(diff_full[j, rows], rot, j, acc, rows)

    def prepare(c, j):
        rows = rows_of(c, tokens)

        def body(i, carry):
            cols = pl.ds(pl.multiple_of(i * TILE, TILE), TILE)
            depth = pl.ds(pl.multiple_of(j * width + i * TILE, TILE), TILE)
            part[j, rows, cols] = contract_last(weighted[rows], rot[depth, :]).astype(BF)
            return carry

        lax.fori_loop(0, width // TILE, body, 0)

    mask = jax.nn.sigmoid(logits[...])
    copies = []
    locals_ = []

    def weigh(c):
        rows = rows_of(c, tokens)
        weighted[rows] = (mask * acc[rows]).astype(BF)

    def exchange(c):
        rows = rows_of(c, tokens)
        for r in (2, 3, 1):
            to = partner(dp, r)
            copies.append(
                send(diff_full.at[to, rows], diff_all.at[r, rows], di_s.at[r, c], di_r.at[r, c], "dp", to)
            )
            copies.append(
                send(weighted.at[rows], weighted_all.at[r, rows], we_s.at[r, c], we_r.at[r, c], "dp", to)
            )
            copies[-2].start()
            copies[-1].start()
        mine = pltpu.make_async_copy(diff_full.at[dp, rows], diff_all.at[0, rows], own_sem.at[0, c])
        ours = pltpu.make_async_copy(weighted.at[rows], weighted_all.at[0, rows], own_sem.at[1, c])
        mine.start()
        ours.start()
        locals_.extend((mine, ours))

    gather, gather_drain = line_gather(diff_full, gd_s, gd_r, me, n, tokens, use)
    reduce, finish, reduce_drain = line_reduce(
        part, sums, red_s, red_r, acc, me, n, tokens, prepare
    )
    spread, spread_drain = line_gather(inter_full, gi_s, gi_r, me, n, tokens, lambda c, j: None)

    def settle(c):
        finish(c)
        rows = rows_of(c, tokens)
        mine = (base[rows].astype(F32) + acc[rows]).astype(BF)
        inter_full[me, rows] = mine
        inter_own[rows] = mine

    for k in range(n - 1):
        gather(0, k)
    gather(1, 0)
    gather(0, n - 1)
    weigh(0)
    for s in range(n - 1):
        reduce(0, s)
        if s == 0:
            exchange(0)
        gather(1, s + 1)
    settle(0)
    spread(0, 0)
    weigh(1)
    for s in range(n - 1):
        reduce(1, s)
        if s == 0:
            exchange(1)
        spread(0, s + 1)
    settle(1)
    for k in range(n):
        spread(1, k)
    for copy in copies:
        copy.wait_recv()
    for copy in locals_:
        copy.wait()
    for copy in copies + [one, two, three]:
        copy.wait_send()
    gather_drain()
    reduce_drain()
    spread_drain()


def recip_of(inter, n):
    tokens, width = inter.shape[1:]
    square = jnp.zeros((tokens, 1), F32)
    for j in range(n):
        block = inter[j].astype(F32)
        square = square + jnp.sum(block * block, axis=1, keepdims=True)
    return lax.rsqrt(square / (n * width) + 1e-05)


def ffn_kernel(n, inter, gain, wg, wu, cot, out, normed, total):
    tokens, width = inter.shape[1:]
    step = pl.program_id(0)

    @pl.when(step == 0)
    def _():
        recip = recip_of(inter, n)
        for j in range(n):
            cols = pl.ds(j * width, width)
            scale = gain[:, cols].astype(F32)
            normed[:, cols] = (inter[j].astype(F32) * recip * scale).astype(BF)
        total[...] = jnp.zeros_like(total)

    gate = jnp.dot(normed[...], wg[...], preferred_element_type=F32)
    up = jnp.dot(normed[...], wu[...], preferred_element_type=F32)
    sig = jax.nn.sigmoid(gate)
    cotan = cot[...].astype(F32)
    dgate = (cotan * up * sig * (1.0 + gate * (1.0 - sig))).astype(BF)
    dup = (cotan * gate * sig).astype(BF)
    for i in range(n * width // 512):
        rows = pl.ds(i * 512, 512)
        total[:, rows] += contract_last(dgate, wg[rows, :]) + contract_last(dup, wu[rows, :])

    @pl.when(step == pl.num_programs(0) - 1)
    def _():
        for j in range(n):
            out[j] = total[:, pl.ds(j * width, width)].astype(BF)


def slot_of(a, b):
    return (a + b) % 2 + 2 * ((a // 2 + b // 2) % 2)


def back_kernel(
    n,
    part,
    inter,
    gain,
    logits,
    rot_hbm,
    dinter_all,
    coupled_all,
    rot,
    sums,
    dn,
    dn_all,
    inter_all,
    dinter,
    acc,
    stat,
    recip,
    aux,
    rot_sem,
    red_s,
    red_r,
    ga_s,
    ga_r,
    in_s,
    in_r,
    dn_s,
    dn_r,
    au_s,
    au_r,
    co_s,
    co_r,
):
    me = lax.axis_index("mp")
    dp = lax.axis_index("dp")
    tokens, width = part.shape[1:]
    near, far = partner(dp, 1), partner(dp, 2)
    load = pltpu.make_async_copy(rot_hbm, rot, rot_sem)
    load.start()
    greet(me, n, dp)

    def use(c, j):
        rows = rows_of(c, tokens)

        @pl.when(j != dp)
        def _():
            r = slot_of(j, dp)
            send(dn.at[j, rows], dn_all.at[r, rows], dn_s.at[r, c], dn_r.at[r, c], "dp", j).start()

        scaled = gain[j].astype(F32) * dn[j, rows].astype(F32)
        stat[rows] += jnp.sum(scaled * inter[j, rows].astype(F32), axis=1, keepdims=True)

    reduce, finish, reduce_drain = line_reduce(part, sums, red_s, red_r, acc, me, n, tokens, None)
    gather, gather_drain = line_gather(dn, ga_s, ga_r, me, n, tokens, use)

    def settle(c):
        finish(c)
        rows = rows_of(c, tokens)
        dn[me, rows] = acc[rows].astype(BF)

    inters, auxes, ones, twos, threes = [], [], [], [], []

    def couple(c):
        rows = rows_of(c, tokens)
        scale = recip[rows]
        coef = scale * scale * scale * stat[rows] / (n * width)
        lane = lax.broadcasted_iota(jnp.int32, (tokens // CHUNKS, 128), 1)
        aux[0, rows] = jnp.where(lane < 64, scale, coef)
        for r in (2, 3, 1):
            copy = send(
                aux.at[0, rows], aux.at[r, rows], au_s.at[r, c], au_r.at[r, c], "dp", partner(dp, r)
            )
            copy.start()
            auxes.append(copy)
        for j in range(n):
            scaled = gain[j].astype(F32) * dn[j, rows].astype(F32)
            dinter[j, rows] = (scale * scaled - inter[j, rows].astype(F32) * coef).astype(BF)
        acc[rows] = jnp.zeros((tokens // CHUNKS, width), F32)
        for j in range(n):
            times_rotation(dinter[j, rows], rot, j, acc, rows)
        coupled_all[0, rows] = (jax.nn.sigmoid(logits[...]) * acc[rows]).astype(BF)
        own = coupled_all.at[0, rows]
        one = send(own, coupled_all.at[2, rows], co_s.at[0, c], co_r.at[0, c], "dp", far)
        two = send(own, coupled_all.at[1, rows], co_s.at[1, c], co_r.at[1, c], "dp", near)
        one.start()
        two.start()
        ones.append(one)
        twos.append(two)

    def relay(c):
        rows = rows_of(c, tokens)
        ones[c].wait_recv()
        three = send(
            coupled_all.at[2, rows], coupled_all.at[3, rows], co_s.at[2, c], co_r.at[2, c], "dp", near
        )
        three.start()
        threes.append(three)

    def rebuild(c):
        rows = rows_of(c, tokens)
        scale_here = gain[dp].astype(F32)
        dinter_all[0, rows] = dinter[dp, rows]
        for i, r in enumerate((2, 3, 1)):
            auxes[3 * c + i].wait_recv()
            view = dn_all.at[r, rows]
            send(view, view, dn_s.at[r, c], dn_r.at[r, c], "dp", partner(dp, r)).wait_recv()
            scaled = scale_here * dn_all[r, rows].astype(F32)
            scale, coef = aux[r, rows, 0:1], aux[r, rows, 64:65]
            dinter_all[r, rows] = (
                scale * scaled - inter_all[r, rows].astype(F32) * coef
            ).astype(BF)

    stat[...] = jnp.zeros_like(stat)
    for s in range(n - 1):
        reduce(0, s)
        if s == 0:
            for r in (2, 3, 1):
                to = partner(dp, r)
                copy = send(inter.at[to], inter_all.at[r], in_s.at[r], in_r.at[r], "dp", to)
                copy.start()
                inters.append(copy)
            recip[...] = recip_of(inter, n)
    reduce(1, 0)
    settle(0)
    for k in range(n - 1):
        gather(0, k)
        if k + 1 < n - 1:
            reduce(1, k + 1)
    settle(1)
    gather(1, 0)
    gather(0, n - 1)
    gather(1, 1)
    load.wait()
    couple(0)
    for k in range(2, n):
        gather(1, k)
    couple(1)
    relay(0)
    for copy in inters:
        copy.wait_recv()
    rebuild(0)
    relay(1)
    rebuild(1)
    for copy in twos + threes:
        copy.wait_recv()
    for copy in inters + auxes + ones + twos + threes:
        copy.wait_send()
    for r in (1, 2, 3):
        for c in range(CHUNKS):
            view = dn_all.at[r, rows_of(c, tokens)]
            send(view, view, dn_s.at[r, c], dn_r.at[r, c], "dp", partner(dp, r)).wait_send()
    reduce_drain()
    gather_drain()


def grad_kernel(count, dinter, coupled, weighted, diff, out):
    acc = jnp.zeros(out.shape, F32)
    for r in range(count):
        acc = acc + contract_first(dinter[r], weighted[r])
        acc = acc + contract_first(diff[r], coupled[r])
    out[...] = acc


def vmem():
    return pl.BlockSpec(memory_space=pltpu.VMEM)


def anywhere():
    return pl.BlockSpec(memory_space=pl.ANY)


def dma(*shape):
    return pltpu.SemaphoreType.DMA(shape)


def fast(
    n,
    base_states,
    source_states,
    source_rank,
    source_row,
    rotation,
    mask_logits,
    norm_gain,
    gate_weight,
    up_weight,
    hidden_cot,
):
    tokens, width = base_states.shape
    hidden = gate_weight.shape[1]
    full = rotation.shape[0]
    peers = 4
    index = source_rank * tokens + source_row[:, None]
    logits = mask_logits[None, :]
    whole = jax.ShapeDtypeStruct((n, tokens, width), BF)
    one = jax.ShapeDtypeStruct((tokens, width), BF)
    line = (2, n - 1, CHUNKS)
    spread = jax.ShapeDtypeStruct((peers, tokens, width), BF)
    weighted_all, diff_all, inter_full, interchanged = pl.pallas_call(
        functools.partial(front_kernel, n),
        out_shape=(spread, spread, whole, one),
        in_specs=[vmem()] * 4 + [anywhere()],
        out_specs=(anywhere(), anywhere(), vmem(), vmem()),
        scratch_shapes=[
            pltpu.VMEM((full, width), BF),
            pltpu.VMEM((peers, tokens, width), BF),
            pltpu.VMEM((n, tokens, width), BF),
            pltpu.VMEM((tokens, width), BF),
            pltpu.VMEM((n, tokens, width), BF),
            pltpu.VMEM((2, n, tokens, width), BF),
            pltpu.VMEM((tokens, width), F32),
            pltpu.SemaphoreType.DMA,
            dma(2, CHUNKS),
            dma(3),
            dma(3),
            dma(*line),
            dma(*line),
            dma(2, n, CHUNKS),
            dma(2, n, CHUNKS),
            dma(*line),
            dma(*line),
            dma(peers, CHUNKS),
            dma(peers, CHUNKS),
            dma(peers, CHUNKS),
            dma(peers, CHUNKS),
        ],
        compiler_params=pltpu.CompilerParams(collective_id=0, has_side_effects=True),
        name="front",
    )(source_states, base_states, index, logits, rotation)

    block = 512 if hidden % 512 == 0 else hidden
    part = pl.pallas_call(
        functools.partial(ffn_kernel, n),
        out_shape=whole,
        grid=(hidden // block,),
        in_specs=[
            pl.BlockSpec((n, tokens, width), lambda i: (0, 0, 0)),
            pl.BlockSpec((1, full), lambda i: (0, 0)),
            pl.BlockSpec((full, block), lambda i: (0, i)),
            pl.BlockSpec((full, block), lambda i: (0, i)),
            pl.BlockSpec((tokens, block), lambda i: (0, i)),
        ],
        out_specs=pl.BlockSpec((n, tokens, width), lambda i: (0, 0, 0)),
        scratch_shapes=[pltpu.VMEM((tokens, full), BF), pltpu.VMEM((tokens, full), F32)],
        cost_estimate=pl.CostEstimate(
            flops=8 * tokens * full * hidden,
            bytes_accessed=4 * full * hidden,
            transcendentals=tokens * hidden,
        ),
        name="ffn",
    )(inter_full, norm_gain[None, :], gate_weight, up_weight, hidden_cot)

    dinter_all, coupled_all = pl.pallas_call(
        functools.partial(back_kernel, n),
        out_shape=(jax.ShapeDtypeStruct((peers, tokens, width), BF),) * 2,
        in_specs=[vmem()] * 4 + [anywhere()],
        out_specs=(vmem(),) * 2,
        scratch_shapes=[
            pltpu.VMEM((full, width), BF),
            pltpu.VMEM((2, n, tokens, width), BF),
            pltpu.VMEM((n, tokens, width), BF),
            pltpu.VMEM((peers, tokens, width), BF),
            pltpu.VMEM((peers, tokens, width), BF),
            pltpu.VMEM((n, tokens, width), BF),
            pltpu.VMEM((tokens, width), F32),
            pltpu.VMEM((tokens, 1), F32),
            pltpu.VMEM((tokens, 1), F32),
            pltpu.VMEM((peers, tokens, 128), F32),
            pltpu.SemaphoreType.DMA,
            dma(2, n, CHUNKS),
            dma(2, n, CHUNKS),
            dma(*line),
            dma(*line),
            dma(peers),
            dma(peers),
            dma(peers, CHUNKS),
            dma(peers, CHUNKS),
            dma(peers, CHUNKS),
            dma(peers, CHUNKS),
            dma(3, CHUNKS),
            dma(3, CHUNKS),
        ],
        compiler_params=pltpu.CompilerParams(collective_id=1, has_side_effects=True),
        name="back",
    )(part, inter_full, norm_gain.reshape(n, 1, width), logits, rotation)

    rows = 256
    rotation_grad = pl.pallas_call(
        functools.partial(grad_kernel, peers),
        out_shape=jax.ShapeDtypeStruct((full // peers, width), F32),
        grid=(full // peers // rows,),
        in_specs=[
            pl.BlockSpec((peers, tokens, rows), lambda i: (0, 0, i)),
            pl.BlockSpec((peers, tokens, width), lambda i: (0, 0, 0)),
            pl.BlockSpec((peers, tokens, width), lambda i: (0, 0, 0)),
            pl.BlockSpec((peers, tokens, rows), lambda i: (0, 0, i)),
        ],
        out_specs=pl.BlockSpec((rows, width), lambda i: (i, 0)),
        name="grad",
    )(dinter_all, coupled_all, weighted_all, diff_all)
    return (rotation_grad, interchanged)


def plain(
    base_states,
    source_states,
    source_rank,
    source_row,
    rotation,
    mask_logits,
    norm_gain,
    gate_weight,
    up_weight,
    hidden_cot,
):
    tokens = base_states.shape[0]
    width = rotation.shape[0]
    ranks_of = source_rank[:, 0]
    everyone = lax.all_gather(source_states, "dp", axis=0, tiled=True)
    paired = jnp.take(everyone, ranks_of * tokens + source_row, axis=0)
    diff_local = (paired.astype(jnp.float32) - base_states.astype(jnp.float32)).astype(jnp.bfloat16)
    diff_full = lax.all_gather(diff_local, "mp", axis=1, tiled=True)
    mask = jax.nn.sigmoid(mask_logits)[None, :]
    coords = jnp.dot(diff_full, rotation, preferred_element_type=jnp.float32)
    weighted = (mask * coords).astype(jnp.bfloat16)
    moved = lax.psum_scatter(
        contract_last(rotation, weighted), "mp", scatter_dimension=0, tiled=True
    ).T
    interchanged = (base_states.astype(jnp.float32) + moved).astype(jnp.bfloat16)
    full_rows = lax.all_gather(interchanged, "mp", axis=1, tiled=True)
    states = full_rows.astype(jnp.float32)
    gain_f = norm_gain.astype(jnp.float32)[None, :]
    recip = lax.rsqrt(jnp.mean(states * states, axis=1, keepdims=True) + 1e-05)
    normed = (states * recip * gain_f).astype(jnp.bfloat16)
    gate = jnp.dot(normed, gate_weight, preferred_element_type=jnp.float32)
    up_val = jnp.dot(normed, up_weight, preferred_element_type=jnp.float32)
    sigm = jax.nn.sigmoid(gate)
    cotan = hidden_cot.astype(jnp.float32)
    dgate = (cotan * up_val * sigm * (1.0 + gate * (1.0 - sigm))).astype(jnp.bfloat16)
    dup_val = (cotan * gate * sigm).astype(jnp.bfloat16)
    partial_grad = contract_last(dgate, gate_weight) + contract_last(dup_val, up_weight)
    dnormed = lax.psum(partial_grad, "mp")
    scaled = gain_f * dnormed
    stat = jnp.sum(scaled * states, axis=1, keepdims=True)
    dinter = (recip * scaled - states * recip * recip * recip * stat / width).astype(jnp.bfloat16)
    coupled = (mask * jnp.dot(dinter, rotation, preferred_element_type=jnp.float32)).astype(
        jnp.bfloat16
    )
    rotation_grad = lax.psum_scatter(
        (contract_first(dinter, weighted) + contract_first(diff_full, coupled)).astype(
            jnp.bfloat16
        ),
        "dp",
        scatter_dimension=0,
        tiled=True,
    ).astype(jnp.float32)
    return (rotation_grad, interchanged)


def solution(mesh):
    n = mesh.shape["mp"]

    def shards(*args):
        width = args[0].shape[1]
        tokens = args[0].shape[0]
        full = args[4].shape[0]
        fits = (
            width % TILE == 0
            and mesh.shape["dp"] == 4
            and n == 4
            and n * width == full
            and full // 4 == width
            and tokens % (16 * CHUNKS) == 0
        )
        if fits:
            return fast(n, *args)
        return plain(*args)

    placed = (
        P(("groups", "dp"), "mp"),
        P(("groups", "dp"), "mp"),
        P(("groups", "dp"), None),
        P(("groups", "dp")),
        P(None, "mp"),
        P("mp"),
        P(),
        P(None, "mp"),
        P(None, "mp"),
        P(("groups", "dp"), "mp"),
    )
    return jax.shard_map(
        shards,
        mesh=mesh,
        in_specs=placed,
        out_specs=(P(("groups", "dp"), "mp"), P(("groups", "dp"), "mp")),
        check_vma=False,
    )
```

```python
import functools

import jax
import jax.numpy as jnp
from jax import lax
from jax.experimental import pallas as pl
from jax.experimental.pallas import tpu as pltpu
from jax.sharding import PartitionSpec as P

BF = jnp.bfloat16
F32 = jnp.float32
CHUNKS = 2
TILE = 512


def contract_first(left, right):
    return lax.dot_general(
        left, right, (((0,), (0,)), ((), ())), preferred_element_type=F32
    )


def contract_last(left, right):
    return lax.dot_general(
        left, right, (((1,), (1,)), ((), ())), preferred_element_type=F32
    )


def send(src, dst, ssem, rsem, axis, dev):
    return pltpu.make_async_remote_copy(
        src_ref=src,
        dst_ref=dst,
        send_sem=ssem,
        recv_sem=rsem,
        device_id={axis: dev},
        device_id_type=pl.DeviceIdType.MESH,
    )


def rows_of(chunk, tokens):
    size = tokens // CHUNKS
    return pl.ds(chunk * size, size)


def greet(me, n, dp):
    barrier = pltpu.get_barrier_semaphore()
    for r in (1, 2, 3):
        pl.semaphore_signal(
            barrier, inc=1, device_id={"dp": partner(dp, r)}, device_id_type=pl.DeviceIdType.MESH
        )

    @pl.when(me > 0)
    def _():
        pl.semaphore_signal(
            barrier, inc=1, device_id={"mp": me - 1}, device_id_type=pl.DeviceIdType.MESH
        )

    @pl.when(me < n - 1)
    def _():
        pl.semaphore_signal(
            barrier, inc=1, device_id={"mp": me + 1}, device_id_type=pl.DeviceIdType.MESH
        )

    pl.semaphore_wait(barrier, 3 + jnp.minimum(me, 1) + jnp.minimum(n - 1 - me, 1))


def partner(dp, r):
    low = dp % 2
    high = dp // 2
    if r % 2:
        low = 1 - low
    if r // 2:
        high = 1 - high
    return high * 2 + low


def line_gather(buf, ssem, rsem, me, n, tokens, use):
    def hop(way, k, c):
        shard, to = (me - k, me + 1) if way == 0 else (me + k, me - 1)
        view = buf.at[shard, rows_of(c, tokens)]
        return send(view, view, ssem.at[way, k, c], rsem.at[way, k, c], "mp", to)

    def arrival(way, k, c):
        shard, frm = (me - 1 - k, me - 1) if way == 0 else (me + 1 + k, me + 1)
        view = buf.at[shard, rows_of(c, tokens)]
        return send(view, view, ssem.at[way, k, c], rsem.at[way, k, c], "mp", frm)

    def sends(way, k):
        if way == 0:
            return (me - k >= 0) & (me < n - 1)
        return (me + k <= n - 1) & (me > 0)

    def step(c, k):
        here = (me - k >= 0, me + k <= n - 1)
        for way in (0, 1):
            if k > 0:
                pl.when(here[way])(lambda: arrival(way, k - 1, c).wait_recv())
            if k < n - 1:
                pl.when(sends(way, k))(lambda: hop(way, k, c).start())
        if k == 0:
            use(c, me)
        else:
            pl.when(here[0])(lambda: use(c, me - k))
            pl.when(here[1])(lambda: use(c, me + k))

    def drain():
        for k in range(n - 1):
            for c in range(CHUNKS):
                for way in (0, 1):
                    pl.when(sends(way, k))(lambda: hop(way, k, c).wait_send())

    return step, drain


def line_reduce(part, sums, ssem, rsem, total, me, n, tokens, prepare):
    flip = (me * 2) // n
    sign = 1 - 2 * flip
    v = me + flip * (n - 1 - 2 * me)

    def real(j):
        return j + flip * (n - 1 - 2 * j)

    def hop(stream, j, c):
        way = flip if stream == 0 else 1 - flip
        to = me + sign if stream == 0 else me - sign
        view = sums.at[way, real(j), rows_of(c, tokens)]
        return send(view, view, ssem.at[way, real(j), c], rsem.at[way, real(j), c], "mp", to)

    def one(stream, j, c):
        way = flip if stream == 0 else 1 - flip
        rows = rows_of(c, tokens)
        first = (v == 0) if stream == 0 else (v == n - 1)
        sender = (v < j) if stream == 0 else (v > j)

        @pl.when(sender & first)
        def _():
            sums[way, real(j), rows] = part[real(j), rows]

        @pl.when(sender & jnp.logical_not(first))
        def _():
            hop(stream, j, c).wait_recv()
            sums[way, real(j), rows] = (
                sums[way, real(j), rows].astype(F32) + part[real(j), rows].astype(F32)
            ).astype(BF)

        pl.when(sender)(lambda: hop(stream, j, c).start())

    def step(c, s):
        for stream, j in ((0, n - 1 - s), (1, s)):
            if prepare is not None and s <= n - 1 - s and (stream == 0 or s < n - 1 - s):
                prepare(c, real(j))
            one(stream, j, c)

    def finish(c):
        rows = rows_of(c, tokens)
        total[rows] = part[me, rows].astype(F32)
        for way, there, frm in ((0, me > 0, me - 1), (1, me < n - 1, me + 1)):

            @pl.when(there)
            def _():
                view = sums.at[way, me, rows]
                send(view, view, ssem.at[way, me, c], rsem.at[way, me, c], "mp", frm).wait_recv()
                total[rows] += sums[way, me, rows].astype(F32)

    def drain():
        for s in range(n - 1):
            for stream, j in ((0, n - 1 - s), (1, s)):
                sender = (v < j) if stream == 0 else (v > j)
                for c in range(CHUNKS):
                    pl.when(sender)(lambda: hop(stream, j, c).wait_send())

    return step, finish, drain


def times_rotation(left, rot, block, acc, rows):
    shard = left.shape[1]

    def body(i, carry):
        cols = pl.ds(pl.multiple_of(i * TILE, TILE), TILE)
        depth = pl.ds(pl.multiple_of(block * shard, shard), shard)
        acc[rows, cols] += jnp.dot(left, rot[depth, cols], preferred_element_type=F32)
        return carry

    lax.fori_loop(0, acc.shape[1] // TILE, body, 0)


def front_kernel(
    n,
    src,
    base,
    index,
    logits,
    rot_hbm,
    weighted_all,
    diff_all,
    inter_full,
    inter_own,
    rot,
    pool,
    diff_full,
    weighted,
    part,
    sums,
    acc,
    rot_sem,
    own_sem,
    pool_s,
    pool_r,
    gd_s,
    gd_r,
    red_s,
    red_r,
    gi_s,
    gi_r,
    di_s,
    di_r,
    we_s,
    we_r,
):
    me = lax.axis_index("mp")
    dp = lax.axis_index("dp")
    tokens, width = src.shape
    load = pltpu.make_async_copy(rot_hbm, rot, rot_sem)
    load.start()
    greet(me, n, dp)

    def across(i, frm, to):
        return send(frm, pool.at[to[0]], pool_s.at[i], pool_r.at[i], "dp", to[1])

    near, far, both = partner(dp, 1), partner(dp, 2), partner(dp, 3)
    one = across(0, src, (2, far))
    two = across(1, src, (1, near))
    one.start()
    two.start()
    owner = index[...]
    lane = lax.broadcasted_iota(jnp.int32, (tokens, tokens), 1)

    def pick(rows_in, who):
        hit = (owner == lane + who * tokens).astype(F32).astype(BF)
        return jnp.dot(hit, rows_in, preferred_element_type=F32)

    acc[...] = pick(src[...], dp)
    two.wait_recv()
    acc[...] += pick(pool[1], near)
    one.wait_recv()
    three = across(2, pool.at[2], (3, near))
    three.start()
    acc[...] += pick(pool[2], far)
    three.wait_recv()
    acc[...] += pick(pool[3], both)
    diff_full[me] = (acc[...] - base[...].astype(F32)).astype(BF)
    acc[...] = jnp.zeros_like(acc)

    waited = []

    def use(c, j):
        if not waited:
            waited.append(True)
            load.wait()
        rows = rows_of(c, tokens)
        times_rotation(diff_full[j, rows], rot, j, acc, rows)

    def prepare(c, j):
        rows = rows_of(c, tokens)

        def body(i, carry):
            cols = pl.ds(pl.multiple_of(i * TILE, TILE), TILE)
            depth = pl.ds(pl.multiple_of(j * width + i * TILE, TILE), TILE)
            part[j, rows, cols] = contract_last(weighted[rows], rot[depth, :]).astype(BF)
            return carry

        lax.fori_loop(0, width // TILE, body, 0)

    mask = jax.nn.sigmoid(logits[...])
    copies = []
    locals_ = []

    def weigh(c):
        rows = rows_of(c, tokens)
        weighted[rows] = (mask * acc[rows]).astype(BF)

    def exchange(c):
        rows = rows_of(c, tokens)
        for r in (2, 3, 1):
            to = partner(dp, r)
            copies.append(
                send(diff_full.at[to, rows], diff_all.at[r, rows], di_s.at[r, c], di_r.at[r, c], "dp", to)
            )
            copies.append(
                send(weighted.at[rows], weighted_all.at[r, rows], we_s.at[r, c], we_r.at[r, c], "dp", to)
            )
            copies[-2].start()
            copies[-1].start()
        mine = pltpu.make_async_copy(diff_full.at[dp, rows], diff_all.at[0, rows], own_sem.at[0, c])
        ours = pltpu.make_async_copy(weighted.at[rows], weighted_all.at[0, rows], own_sem.at[1, c])
        mine.start()
        ours.start()
        locals_.extend((mine, ours))

    gather, gather_drain = line_gather(diff_full, gd_s, gd_r, me, n, tokens, use)
    reduce, finish, reduce_drain = line_reduce(
        part, sums, red_s, red_r, acc, me, n, tokens, prepare
    )
    spread, spread_drain = line_gather(inter_full, gi_s, gi_r, me, n, tokens, lambda c, j: None)

    def settle(c):
        finish(c)
        rows = rows_of(c, tokens)
        mine = (base[rows].astype(F32) + acc[rows]).astype(BF)
        inter_full[me, rows] = mine
        inter_own[rows] = mine

    for k in range(n - 1):
        gather(0, k)
    gather(1, 0)
    gather(0, n - 1)
    weigh(0)
    for s in range(n - 1):
        reduce(0, s)
        if s == 0:
            exchange(0)
        gather(1, s + 1)
    settle(0)
    spread(0, 0)
    weigh(1)
    for s in range(n - 1):
        reduce(1, s)
        if s == 0:
            exchange(1)
        spread(0, s + 1)
    settle(1)
    for k in range(n):
        spread(1, k)
    for copy in copies:
        copy.wait_recv()
    for copy in locals_:
        copy.wait()
    for copy in copies + [one, two, three]:
        copy.wait_send()
    gather_drain()
    reduce_drain()
    spread_drain()


def recip_of(inter, n):
    tokens, width = inter.shape[1:]
    square = jnp.zeros((tokens, 1), F32)
    for j in range(n):
        block = inter[j].astype(F32)
        square = square + jnp.sum(block * block, axis=1, keepdims=True)
    return lax.rsqrt(square / (n * width) + 1e-05)


def ffn_kernel(n, inter, gain, wg, wu, cot, dgate, dup, normed):
    tokens, width = inter.shape[1:]

    @pl.when(pl.program_id(0) == 0)
    def _():
        recip = recip_of(inter, n)
        for j in range(n):
            cols = pl.ds(j * width, width)
            scale = gain[:, cols].astype(F32)
            normed[:, cols] = (inter[j].astype(F32) * recip * scale).astype(BF)

    gate = jnp.dot(normed[...], wg[...], preferred_element_type=F32)
    up = jnp.dot(normed[...], wu[...], preferred_element_type=F32)
    sig = jax.nn.sigmoid(gate)
    cotan = cot[...].astype(F32)
    dgate[...] = (cotan * up * sig * (1.0 + gate * (1.0 - sig))).astype(BF)
    dup[...] = (cotan * gate * sig).astype(BF)


def slot_of(a, b):
    return (a + b) % 2 + 2 * ((a // 2 + b // 2) % 2)


def back_kernel(
    n,
    dgate,
    dup,
    inter,
    gain,
    logits,
    rot_hbm,
    wg,
    wu,
    dinter_all,
    coupled_all,
    rot,
    part,
    blocks,
    sums,
    dn,
    dn_all,
    inter_all,
    dinter,
    acc,
    stat,
    recip,
    aux,
    rot_sem,
    block_sem,
    red_s,
    red_r,
    ga_s,
    ga_r,
    in_s,
    in_r,
    dn_s,
    dn_r,
    au_s,
    au_r,
    co_s,
    co_r,
):
    me = lax.axis_index("mp")
    dp = lax.axis_index("dp")
    tokens, width = inter.shape[1:]
    near, far = partner(dp, 1), partner(dp, 2)
    load = pltpu.make_async_copy(rot_hbm, rot, rot_sem)
    size = blocks.shape[2]
    per = width // size

    def fetch(row, slot):
        rows = pl.ds(pl.multiple_of(row, size), size)
        return (
            pltpu.make_async_copy(wg.at[rows, :], blocks.at[slot, 0], block_sem.at[slot, 0]),
            pltpu.make_async_copy(wu.at[rows, :], blocks.at[slot, 1], block_sem.at[slot, 1]),
        )

    flip = (me * 2) // n
    order = []
    for s in range(n // 2):
        for j in (n - 1 - s, s):
            order.append(j + flip * (n - 1 - 2 * j))
    for copy in fetch(order[0] * width, 0):
        copy.start()
    greet(me, n, dp)
    done = []

    def prepare(c, j):
        if c > 0:
            return
        p = len(done)
        done.append(p)
        here = order[p]
        after = order[p + 1] if p + 1 < n else None

        def body(i, carry):
            slot = i % 2
            if after is not None:
                end = (i + 1) // per
                row = (here * width + (i + 1) * size) * (1 - end) + after * width * end
                for copy in fetch(row, 1 - slot):
                    copy.start()
            else:

                @pl.when(i + 1 < per)
                def _():
                    for copy in fetch(here * width + (i + 1) * size, 1 - slot):
                        copy.start()

            for copy in fetch(here * width + i * size, slot):
                copy.wait()
            cols = pl.ds(pl.multiple_of(i * size, size), size)
            part[here, :, cols] = (
                contract_last(dgate[...], blocks[slot, 0])
                + contract_last(dup[...], blocks[slot, 1])
            ).astype(BF)
            return carry

        lax.fori_loop(0, per, body, 0)

    def use(c, j):
        rows = rows_of(c, tokens)

        @pl.when(j != dp)
        def _():
            r = slot_of(j, dp)
            send(dn.at[j, rows], dn_all.at[r, rows], dn_s.at[r, c], dn_r.at[r, c], "dp", j).start()

        scaled = gain[j].astype(F32) * dn[j, rows].astype(F32)
        stat[rows] += jnp.sum(scaled * inter[j, rows].astype(F32), axis=1, keepdims=True)

    reduce, finish, reduce_drain = line_reduce(part, sums, red_s, red_r, acc, me, n, tokens, prepare)
    gather, gather_drain = line_gather(dn, ga_s, ga_r, me, n, tokens, use)

    def settle(c):
        finish(c)
        rows = rows_of(c, tokens)
        dn[me, rows] = acc[rows].astype(BF)

    inters, auxes, ones, twos, threes = [], [], [], [], []

    def couple(c):
        rows = rows_of(c, tokens)
        scale = recip[rows]
        coef = scale * scale * scale * stat[rows] / (n * width)
        lane = lax.broadcasted_iota(jnp.int32, (tokens // CHUNKS, 128), 1)
        aux[0, rows] = jnp.where(lane < 64, scale, coef)
        for r in (2, 3, 1):
            copy = send(
                aux.at[0, rows], aux.at[r, rows], au_s.at[r, c], au_r.at[r, c], "dp", partner(dp, r)
            )
            copy.start()
            auxes.append(copy)
        for j in range(n):
            scaled = gain[j].astype(F32) * dn[j, rows].astype(F32)
            dinter[j, rows] = (scale * scaled - inter[j, rows].astype(F32) * coef).astype(BF)
        acc[rows] = jnp.zeros((tokens // CHUNKS, width), F32)
        for j in range(n):
            times_rotation(dinter[j, rows], rot, j, acc, rows)
        coupled_all[0, rows] = (jax.nn.sigmoid(logits[...]) * acc[rows]).astype(BF)
        own = coupled_all.at[0, rows]
        one = send(own, coupled_all.at[2, rows], co_s.at[0, c], co_r.at[0, c], "dp", far)
        two = send(own, coupled_all.at[1, rows], co_s.at[1, c], co_r.at[1, c], "dp", near)
        one.start()
        two.start()
        ones.append(one)
        twos.append(two)

    def relay(c):
        rows = rows_of(c, tokens)
        ones[c].wait_recv()
        three = send(
            coupled_all.at[2, rows], coupled_all.at[3, rows], co_s.at[2, c], co_r.at[2, c], "dp", near
        )
        three.start()
        threes.append(three)

    def rebuild(c):
        rows = rows_of(c, tokens)
        scale_here = gain[dp].astype(F32)
        dinter_all[0, rows] = dinter[dp, rows]
        for i, r in enumerate((2, 3, 1)):
            auxes[3 * c + i].wait_recv()
            view = dn_all.at[r, rows]
            send(view, view, dn_s.at[r, c], dn_r.at[r, c], "dp", partner(dp, r)).wait_recv()
            scaled = scale_here * dn_all[r, rows].astype(F32)
            scale, coef = aux[r, rows, 0:1], aux[r, rows, 64:65]
            dinter_all[r, rows] = (
                scale * scaled - inter_all[r, rows].astype(F32) * coef
            ).astype(BF)

    stat[...] = jnp.zeros_like(stat)
    for s in range(n - 1):
        reduce(0, s)
        if s == 0:
            for r in (2, 3, 1):
                to = partner(dp, r)
                copy = send(inter.at[to], inter_all.at[r], in_s.at[r], in_r.at[r], "dp", to)
                copy.start()
                inters.append(copy)
            recip[...] = recip_of(inter, n)
    load.start()
    reduce(1, 0)
    settle(0)
    for k in range(n - 1):
        gather(0, k)
        if k + 1 < n - 1:
            reduce(1, k + 1)
    settle(1)
    gather(1, 0)
    gather(0, n - 1)
    gather(1, 1)
    load.wait()
    couple(0)
    for k in range(2, n):
        gather(1, k)
    couple(1)
    relay(0)
    for copy in inters:
        copy.wait_recv()
    rebuild(0)
    relay(1)
    rebuild(1)
    for copy in twos + threes:
        copy.wait_recv()
    for copy in inters + auxes + ones + twos + threes:
        copy.wait_send()
    for r in (1, 2, 3):
        for c in range(CHUNKS):
            view = dn_all.at[r, rows_of(c, tokens)]
            send(view, view, dn_s.at[r, c], dn_r.at[r, c], "dp", partner(dp, r)).wait_send()
    reduce_drain()
    gather_drain()


def grad_kernel(count, dinter, coupled, weighted, diff, out):
    acc = jnp.zeros(out.shape, F32)
    for r in range(count):
        acc = acc + contract_first(dinter[r], weighted[r])
        acc = acc + contract_first(diff[r], coupled[r])
    out[...] = acc


def vmem():
    return pl.BlockSpec(memory_space=pltpu.VMEM)


def anywhere():
    return pl.BlockSpec(memory_space=pl.ANY)


def dma(*shape):
    return pltpu.SemaphoreType.DMA(shape)


def fast(
    n,
    base_states,
    source_states,
    source_rank,
    source_row,
    rotation,
    mask_logits,
    norm_gain,
    gate_weight,
    up_weight,
    hidden_cot,
):
    tokens, width = base_states.shape
    hidden = gate_weight.shape[1]
    full = rotation.shape[0]
    peers = 4
    index = source_rank * tokens + source_row[:, None]
    logits = mask_logits[None, :]
    whole = jax.ShapeDtypeStruct((n, tokens, width), BF)
    one = jax.ShapeDtypeStruct((tokens, width), BF)
    line = (2, n - 1, CHUNKS)
    spread = jax.ShapeDtypeStruct((peers, tokens, width), BF)
    weighted_all, diff_all, inter_full, interchanged = pl.pallas_call(
        functools.partial(front_kernel, n),
        out_shape=(spread, spread, whole, one),
        in_specs=[vmem()] * 4 + [anywhere()],
        out_specs=(anywhere(), anywhere(), vmem(), vmem()),
        scratch_shapes=[
            pltpu.VMEM((full, width), BF),
            pltpu.VMEM((peers, tokens, width), BF),
            pltpu.VMEM((n, tokens, width), BF),
            pltpu.VMEM((tokens, width), BF),
            pltpu.VMEM((n, tokens, width), BF),
            pltpu.VMEM((2, n, tokens, width), BF),
            pltpu.VMEM((tokens, width), F32),
            pltpu.SemaphoreType.DMA,
            dma(2, CHUNKS),
            dma(3),
            dma(3),
            dma(*line),
            dma(*line),
            dma(2, n, CHUNKS),
            dma(2, n, CHUNKS),
            dma(*line),
            dma(*line),
            dma(peers, CHUNKS),
            dma(peers, CHUNKS),
            dma(peers, CHUNKS),
            dma(peers, CHUNKS),
        ],
        compiler_params=pltpu.CompilerParams(collective_id=0, has_side_effects=True),
        name="front",
    )(source_states, base_states, index, logits, rotation)

    block = 512 if hidden % 512 == 0 else hidden
    dgate, dup = pl.pallas_call(
        functools.partial(ffn_kernel, n),
        out_shape=(jax.ShapeDtypeStruct((tokens, hidden), BF),) * 2,
        grid=(hidden // block,),
        in_specs=[
            pl.BlockSpec((n, tokens, width), lambda i: (0, 0, 0)),
            pl.BlockSpec((1, full), lambda i: (0, 0)),
            pl.BlockSpec((full, block), lambda i: (0, i)),
            pl.BlockSpec((full, block), lambda i: (0, i)),
            pl.BlockSpec((tokens, block), lambda i: (0, i)),
        ],
        out_specs=(pl.BlockSpec((tokens, block), lambda i: (0, i)),) * 2,
        scratch_shapes=[pltpu.VMEM((tokens, full), BF)],
        name="ffn",
    )(inter_full, norm_gain[None, :], gate_weight, up_weight, hidden_cot)

    dinter_all, coupled_all = pl.pallas_call(
        functools.partial(back_kernel, n),
        out_shape=(jax.ShapeDtypeStruct((peers, tokens, width), BF),) * 2,
        in_specs=[vmem()] * 5 + [anywhere()] * 3,
        out_specs=(vmem(),) * 2,
        scratch_shapes=[
            pltpu.VMEM((full, width), BF),
            pltpu.VMEM((n, tokens, width), BF),
            pltpu.VMEM((2, 2, 256, hidden), BF),
            pltpu.VMEM((2, n, tokens, width), BF),
            pltpu.VMEM((n, tokens, width), BF),
            pltpu.VMEM((peers, tokens, width), BF),
            pltpu.VMEM((peers, tokens, width), BF),
            pltpu.VMEM((n, tokens, width), BF),
            pltpu.VMEM((tokens, width), F32),
            pltpu.VMEM((tokens, 1), F32),
            pltpu.VMEM((tokens, 1), F32),
            pltpu.VMEM((peers, tokens, 128), F32),
            pltpu.SemaphoreType.DMA,
            dma(2, 2),
            dma(2, n, CHUNKS),
            dma(2, n, CHUNKS),
            dma(*line),
            dma(*line),
            dma(peers),
            dma(peers),
            dma(peers, CHUNKS),
            dma(peers, CHUNKS),
            dma(peers, CHUNKS),
            dma(peers, CHUNKS),
            dma(3, CHUNKS),
            dma(3, CHUNKS),
        ],
        compiler_params=pltpu.CompilerParams(collective_id=1, has_side_effects=True),
        name="back",
    )(
        dgate,
        dup,
        inter_full,
        norm_gain.reshape(n, 1, width),
        logits,
        rotation,
        gate_weight,
        up_weight,
    )

    rows = 256
    rotation_grad = pl.pallas_call(
        functools.partial(grad_kernel, peers),
        out_shape=jax.ShapeDtypeStruct((full // peers, width), F32),
        grid=(full // peers // rows,),
        in_specs=[
            pl.BlockSpec((peers, tokens, rows), lambda i: (0, 0, i)),
            pl.BlockSpec((peers, tokens, width), lambda i: (0, 0, 0)),
            pl.BlockSpec((peers, tokens, width), lambda i: (0, 0, 0)),
            pl.BlockSpec((peers, tokens, rows), lambda i: (0, 0, i)),
        ],
        out_specs=pl.BlockSpec((rows, width), lambda i: (i, 0)),
        name="grad",
    )(dinter_all, coupled_all, weighted_all, diff_all)
    return (rotation_grad, interchanged)


def plain(
    base_states,
    source_states,
    source_rank,
    source_row,
    rotation,
    mask_logits,
    norm_gain,
    gate_weight,
    up_weight,
    hidden_cot,
):
    tokens = base_states.shape[0]
    width = rotation.shape[0]
    ranks_of = source_rank[:, 0]
    everyone = lax.all_gather(source_states, "dp", axis=0, tiled=True)
    paired = jnp.take(everyone, ranks_of * tokens + source_row, axis=0)
    diff_local = (paired.astype(jnp.float32) - base_states.astype(jnp.float32)).astype(jnp.bfloat16)
    diff_full = lax.all_gather(diff_local, "mp", axis=1, tiled=True)
    mask = jax.nn.sigmoid(mask_logits)[None, :]
    coords = jnp.dot(diff_full, rotation, preferred_element_type=jnp.float32)
    weighted = (mask * coords).astype(jnp.bfloat16)
    moved = lax.psum_scatter(
        contract_last(rotation, weighted), "mp", scatter_dimension=0, tiled=True
    ).T
    interchanged = (base_states.astype(jnp.float32) + moved).astype(jnp.bfloat16)
    full_rows = lax.all_gather(interchanged, "mp", axis=1, tiled=True)
    states = full_rows.astype(jnp.float32)
    gain_f = norm_gain.astype(jnp.float32)[None, :]
    recip = lax.rsqrt(jnp.mean(states * states, axis=1, keepdims=True) + 1e-05)
    normed = (states * recip * gain_f).astype(jnp.bfloat16)
    gate = jnp.dot(normed, gate_weight, preferred_element_type=jnp.float32)
    up_val = jnp.dot(normed, up_weight, preferred_element_type=jnp.float32)
    sigm = jax.nn.sigmoid(gate)
    cotan = hidden_cot.astype(jnp.float32)
    dgate = (cotan * up_val * sigm * (1.0 + gate * (1.0 - sigm))).astype(jnp.bfloat16)
    dup_val = (cotan * gate * sigm).astype(jnp.bfloat16)
    partial_grad = contract_last(dgate, gate_weight) + contract_last(dup_val, up_weight)
    dnormed = lax.psum(partial_grad, "mp")
    scaled = gain_f * dnormed
    stat = jnp.sum(scaled * states, axis=1, keepdims=True)
    dinter = (recip * scaled - states * recip * recip * recip * stat / width).astype(jnp.bfloat16)
    coupled = (mask * jnp.dot(dinter, rotation, preferred_element_type=jnp.float32)).astype(
        jnp.bfloat16
    )
    rotation_grad = lax.psum_scatter(
        (contract_first(dinter, weighted) + contract_first(diff_full, coupled)).astype(
            jnp.bfloat16
        ),
        "dp",
        scatter_dimension=0,
        tiled=True,
    ).astype(jnp.float32)
    return (rotation_grad, interchanged)


def solution(mesh):
    n = mesh.shape["mp"]

    def shards(*args):
        width = args[0].shape[1]
        tokens = args[0].shape[0]
        full = args[4].shape[0]
        fits = (
            width % TILE == 0
            and mesh.shape["dp"] == 4
            and n == 4
            and n * width == full
            and full // 4 == width
            and tokens % (16 * CHUNKS) == 0
        )
        if fits:
            return fast(n, *args)
        return plain(*args)

    placed = (
        P(("groups", "dp"), "mp"),
        P(("groups", "dp"), "mp"),
        P(("groups", "dp"), None),
        P(("groups", "dp")),
        P(None, "mp"),
        P("mp"),
        P(),
        P(None, "mp"),
        P(None, "mp"),
        P(("groups", "dp"), "mp"),
    )
    return jax.shard_map(
        shards,
        mesh=mesh,
        in_specs=placed,
        out_specs=(P(("groups", "dp"), "mp"), P(("groups", "dp"), "mp")),
        check_vma=False,
    )
```
